32 devices in a mesh: region: 8 (over y, x, core), cuts: 4 (over z).
Axes of the slice: x: 2, y: 2, z: 4, core: 2. Of those that a mesh axis runs over, the one named last changes fastest.
Arguments:
- history: bfloat16 [8, 8192, 128], P(None, ('region', 'cuts')), may hold values from -6 to 6
- incident: bfloat16 [4, 8192, 128], P(None, ('region', 'cuts')), may hold values from -6 to 6
- self_inverse: bfloat16 [8192, 256], P(('region', 'cuts')), may hold values from -0.375 to 0.375
- lag_kernels: bfloat16 [384, 8, 256, 256], P(('region', 'cuts')), may hold values from -0.02734375 to 0.02734375
- pair_partner: int32 [384], P(('region', 'cuts')), may hold values from 0 to 11
- pair_lags: int32 [384], P(('region', 'cuts')), may hold values from 1 to 8
Outputs:
- densities: bfloat16 [4, 8192, 128], P(None, ('region', 'cuts'))
The draws below stay inside these ranges and needn't reach their ends.
Inputs may be any that keep to these rules, and one draw needn't show every extreme that they name: `pair_partner`: codes below 4 name a block of the region before the owner's, codes from 8 on one of the region after it, the others one of the owner's region; the same block may be named by several pairs, and a pair's partner may be its owner. Pair p uses lag matrices 1 to pair_lags[p]; the rest are stored but unused.
All inputs are finite; a program needn't handle non-finite values.
Results may differ from the reference program's by a relative error of at most 0.0095.
Values may be sent and summed in bfloat16 or wider, within the bound.
No kernel may reach another device: no remote copies, remote signals or barrier semaphores. Data moves between devices by JAX's collectives and lax.ppermute only.
A program may use at most 128 MiB of HBM per device.

```python
import jax
import jax.numpy as jnp
from jax import lax

P_SIZE = 256
R = 128
LAGS = 8
STEPS = 4
PAIR_DEV = 12
PANELS = 8192
PAIRS = 384
N_REGION = 8
N_CUTS = 4


def set_ends(array, own_key, least, largest):
    index_at = [jax.random.randint(jax.random.fold_in(own_key, axis), (), 0, length) for axis, length in enumerate(array.shape)]
    main_axis = array.shape.index(max(array.shape))
    beside = index_at[:main_axis] + [(index_at[main_axis] + 1) % array.shape[main_axis]] + index_at[main_axis + 1:]
    return array.at[tuple(index_at)].set(least).at[tuple(beside)].set(largest)


def steps_of(stream_key, extent, shards, smallest, largest):
    factor_of = 1.0
    for axis_at, parts in shards:
        steps = jax.random.uniform(jax.random.fold_in(jax.random.fold_in(stream_key, 6), axis_at), (parts,), jnp.float32, smallest / len(shards), largest / len(shards))
        factor_of = factor_of * jnp.repeat(jnp.exp(steps), extent[axis_at] // parts).reshape((-1,) + (1,) * (len(extent) - 1 - axis_at))
    return factor_of


def centred(stream_key, shape, spread, most, split=(), held_as=jnp.bfloat16):
    array = spread * jax.random.normal(stream_key, shape, jnp.float32)
    if split:
        array = array * steps_of(stream_key, shape, split, -0.22, 0.18)
    return jnp.clip(array, -most, most).astype(held_as)


def setup_inputs(seed: int = 0) -> dict:
    key_list = jax.random.split(jax.random.key(seed), 7)
    return {
        "history": centred(key_list[0], (LAGS, PANELS, R), 1.0, 6.0, ((1, 32),)),
        "incident": centred(key_list[1], (STEPS, PANELS, R), 1.0, 6.0, ((1, 32),)),
        "self_inverse": centred(key_list[2], (PANELS, P_SIZE), P_SIZE ** -0.5, 0.375, ((0, 32),)),
        "lag_kernels": centred(key_list[3], (PAIRS, LAGS, P_SIZE, P_SIZE), (P_SIZE * LAGS * PAIR_DEV * 2) ** -0.5, 0.02734375, ((0, 32),)),
        "pair_partner": set_ends(jax.random.randint(key_list[4], (PAIRS,), 0, 3 * N_CUTS), jax.random.fold_in(key_list[4], 1), 0, (3 * N_CUTS) - 1).astype(jnp.int32),
        "pair_lags": set_ends(jax.random.randint(key_list[5], (PAIRS,), 1, LAGS + 1), jax.random.fold_in(key_list[5], 1), 1, LAGS).astype(jnp.int32),
    }


def reference(history, incident, self_inverse, lag_kernels, pair_partner, pair_lags):
    block_count = N_REGION * N_CUTS
    earlier = history.reshape(LAGS, block_count, P_SIZE, R)[::-1]
    timeline = jnp.concatenate([earlier, jnp.zeros((STEPS, block_count, P_SIZE, R), jnp.bfloat16)], axis=0)
    inverses = self_inverse.reshape(block_count, P_SIZE, P_SIZE).astype(jnp.float32)
    kernels = lag_kernels.reshape(block_count, PAIR_DEV, LAGS, P_SIZE, P_SIZE)
    partners = pair_partner.reshape(block_count, PAIR_DEV)
    lag_counts = pair_lags.reshape(block_count, PAIR_DEV)
    incoming = incident.reshape(STEPS, block_count, P_SIZE, R)
    lag_ids = jnp.arange(1, LAGS + 1, dtype=jnp.int32)
    owners = jnp.arange(block_count, dtype=jnp.int32)
    for step_now in range(STEPS):
        window = timeline[step_now:step_now + LAGS][::-1]

        def visit_owner(field_sum, owner_id):
            region_id = owner_id // N_CUTS
            region_step = partners[owner_id] // N_CUTS - 1
            cut_id = partners[owner_id] % N_CUTS
            targets = (((region_id + region_step) % N_REGION) * N_CUTS + cut_id).astype(jnp.int32)
            lag_gate = (lag_ids[None, :] <= lag_counts[owner_id][:, None]).astype(jnp.float32)
            kernel_now = kernels[owner_id].astype(jnp.float32)
            partner_hist = jnp.take(window, targets, axis=1).astype(jnp.float32) * jnp.transpose(lag_gate)[:, :, None, None]
            forward = jnp.einsum("plij,lpjr->ir", kernel_now, partner_hist, precision=lax.Precision.HIGHEST)
            own_hist = lag_gate[:, :, None, None] * window[:, owner_id].astype(jnp.float32)[None]
            backward = jnp.einsum("plij,plir->pjr", kernel_now, own_hist, precision=lax.Precision.HIGHEST)
            field_sum = field_sum.at[owner_id].add(forward)
            field_sum = field_sum.at[targets].add(backward)
            return field_sum, None

        field_sum, _ = lax.scan(visit_owner, jnp.zeros((block_count, P_SIZE, R), jnp.float32), owners)
        excess = (incoming[step_now].astype(jnp.float32) - field_sum).astype(jnp.bfloat16)
        density = jnp.einsum("bij,bjr->bir", inverses, excess.astype(jnp.float32), precision=lax.Precision.HIGHEST).astype(jnp.bfloat16)
        timeline = timeline.at[LAGS + step_now].set(density)
    return timeline[LAGS:].reshape(STEPS, block_count * P_SIZE, R)
```

```python
import functools

import jax
import jax.numpy as jnp
from jax import lax
from jax.experimental import pallas as pl
from jax.experimental.pallas import tpu as pltpu
from jax.sharding import PartitionSpec as P


F32 = jnp.float32
BF16 = jnp.bfloat16
CHUNKS = 3


def dot_nn(a, b):
    return lax.dot_general(a, b, (((1,), (0,)), ((), ())), preferred_element_type=F32)


def dot_nt(a, b):
    return lax.dot_general(a, b, (((1,), (1,)), ((), ())), preferred_element_type=F32)


def even_exchange(value):
    count = lax.axis_size("region")
    return lax.ppermute(value, "region", [(i, i ^ 1) for i in range(count)])


def odd_exchange(value):
    count = lax.axis_size("region")
    route = [(i, (i + 1) % count if i % 2 else (i - 1) % count) for i in range(count)]
    return lax.ppermute(value, "region", route)


def cut_exchange(value, j):
    count = lax.axis_size("cuts")
    return lax.ppermute(value, "cuts", [(i, i ^ j) for i in range(count)])


def whole(shape):
    return pl.BlockSpec(shape, lambda *_: (0,) * len(shape))


def params():
    return pltpu.CompilerParams(vmem_limit_bytes=48 * 1024 * 1024)


def cost(pairs, terms, rows, panels, read):
    return pl.CostEstimate(
        flops=2 * pairs * terms * rows * panels * panels,
        bytes_accessed=read,
        transcendentals=0,
    )


def history_back_body(group, lags, steps, cuts, loc, used, hist, kern, own, even, odd, rest, first):
    step = pl.program_id(0)
    rows = hist.shape[1]
    panels = hist.shape[2]

    @pl.when(step == 0)
    def _():
        first[...] = jnp.zeros_like(first)
        rest[...] = jnp.zeros_like(rest)

    def pair(q, carry):
        slot = loc[step * group + q]

        def lag(l, inner):
            x = hist[pl.ds(lags - l, steps)].reshape(steps * rows, panels)
            y = dot_nn(x, kern[q, l - 1])
            first[slot] += y[:rows]
            rest[slot] += y[rows:]
            return inner

        return lax.fori_loop(1, used[step * group + q] + 1, lag, carry)

    lax.fori_loop(0, group, pair, 0)

    @pl.when(step == pl.num_programs(0) - 1)
    def _():
        own[...] = first[:cuts]
        even[...] = first[cuts : 2 * cuts].astype(BF16)
        odd[...] = first[2 * cuts :].astype(BF16)


def history_back(loc, used, hist, kern, cuts, steps):
    pairs, lags, panels, _ = kern.shape
    rows = hist.shape[1]
    group = max(d for d in (1, 2, 3, 4) if pairs % d == 0)
    part = (cuts, rows, panels)
    rest = (3 * cuts, (steps - 1) * rows, panels)
    return pl.pallas_call(
        functools.partial(history_back_body, group, lags, steps, cuts),
        name="history_back",
        out_shape=(
            jax.ShapeDtypeStruct(part, F32),
            jax.ShapeDtypeStruct(part, BF16),
            jax.ShapeDtypeStruct(part, BF16),
            jax.ShapeDtypeStruct(rest, F32),
        ),
        grid_spec=pltpu.PrefetchScalarGridSpec(
            num_scalar_prefetch=2,
            grid=(pairs // group,),
            in_specs=[
                whole(hist.shape),
                pl.BlockSpec((group, lags, panels, panels), lambda g, *_: (g, 0, 0, 0)),
            ],
            out_specs=(whole(part), whole(part), whole(part), whole(rest)),
            scratch_shapes=[pltpu.VMEM((3 * cuts, rows, panels), F32)],
        ),
        compiler_params=params(),
        cost_estimate=cost(pairs, lags * steps, rows, panels, 2 * kern.size),
    )(loc, used, hist, kern)


def history_front_body(group, lags, steps, cuts, times, loc, used, own, side, even, odd, kern, before, after, near):
    step = pl.program_id(0)
    rows = own.shape[1]
    panels = own.shape[2]
    count = len(times)

    @pl.when(step == 0)
    def _():
        near[0] = own[...]
        near[1:cuts] = side[...]
        near[cuts : 2 * cuts] = even[...]
        near[2 * cuts :] = odd[...]
        after[...] = before[...]

    def pair(q, carry):
        slot = loc[step * group + q]
        last = used[step * group + q]
        for l in range(1, lags + 1):
            met = [i for i, t in enumerate(times) if 0 <= l + t < steps]
            if not met:
                continue
            low, high = met[0], met[-1] + 1
            n = l + times[low]

            @pl.when(l <= last)
            def _(l=l, low=low, high=high, n=n):
                x = near[slot, low:high].reshape((high - low) * rows, panels)
                y = dot_nt(x, kern[q, l - 1])
                after[n : n + high - low] += y.reshape(high - low, rows, panels)

        return carry

    lax.fori_loop(0, group, pair, 0)


def history_front(loc, used, near, kern, before, times):
    own, side, even, odd = near
    pairs, lags, panels, _ = kern.shape
    steps, rows, _ = before.shape
    cuts = even.shape[0]
    group = max(d for d in (1, 2, 3, 4) if pairs % d == 0)
    return pl.pallas_call(
        functools.partial(history_front_body, group, lags, steps, cuts, times),
        name="history_front",
        out_shape=jax.ShapeDtypeStruct(before.shape, F32),
        grid_spec=pltpu.PrefetchScalarGridSpec(
            num_scalar_prefetch=2,
            grid=(pairs // group,),
            in_specs=[
                whole(own.shape),
                whole(side.shape),
                whole(even.shape),
                whole(odd.shape),
                pl.BlockSpec((group, lags, panels, panels), lambda g, *_: (g, 0, 0, 0)),
                whole(before.shape),
            ],
            out_specs=whole(before.shape),
            scratch_shapes=[pltpu.VMEM((3 * cuts, len(times), rows, panels), BF16)],
        ),
        compiler_params=params(),
        cost_estimate=cost(pairs, steps * len(times), rows, panels, 2 * kern.size),
    )(loc, used, own, side, even, odd, kern, before)


def step_body(cuts, pairs, has_front, has_back, loc, *refs):
    refs = list(refs)
    ahead, mine, moved, incoming, inverse, kern = refs[:6]
    refs = refs[6:]
    total = ahead[0] + mine[...]
    for j in range(cuts - 1):
        total = total + moved[j].astype(F32)
    if has_front:
        own, side, even, odd = refs[:4]
        refs = refs[4:]
        near = refs[-1]
        near[0] = own[...]
        near[1:cuts] = side[...]
        near[cuts : 2 * cuts] = even[...]
        near[2 * cuts :] = odd[...]
        for p in range(pairs):
            total = total + dot_nt(near[loc[p]], kern[p, 0])
    excess = (incoming[0].astype(F32) - total).astype(BF16)
    solved = dot_nt(excess, inverse[...])
    density = solved.astype(BF16)
    if has_back:
        begun, out, out_own, out_even, out_odd, sums = refs[:6]
        out[...] = density
        sums[...] = begun[...]
        for p in range(pairs):
            sums[loc[p]] += dot_nn(density, kern[p, 0])
        out_own[...] = sums[:cuts]
        out_even[...] = sums[cuts : 2 * cuts].astype(BF16)
        out_odd[...] = sums[2 * cuts :].astype(BF16)
    else:
        earlier, out = refs[:2]
        count = earlier.shape[0]
        for n in range(count):
            out[n] = earlier[n].astype(F32).T.astype(BF16)
        out[count] = density.astype(F32).T.astype(BF16)


def step_call(n, steps, loc, ahead, mine, moved, incoming, inverse, kern, near, begun, earlier):
    pairs, _, panels, _ = kern.shape
    cuts = moved.shape[0] + 1
    rows = mine.shape[0]
    has_front = near is not None
    has_back = n + 1 < steps
    block = (rows, panels)
    part = (cuts, rows, panels)
    args = [ahead, mine, moved, incoming, inverse, kern]
    specs = [
        pl.BlockSpec((1,) + block, lambda *_: (n, 0, 0)),
        whole(block),
        whole(moved.shape),
        pl.BlockSpec((1,) + block, lambda *_: (n, 0, 0)),
        whole(inverse.shape),
        pl.BlockSpec((pairs, 1, panels, panels), lambda *_: (0, 0, 0, 0)),
    ]
    scratch = []
    if has_front:
        args += list(near)
        specs += [whole(x.shape) for x in near]
    if has_back:
        args.append(begun)
        specs.append(pl.BlockSpec((3 * cuts, rows, panels), lambda *_: (0, n, 0)))
        outs = (
            jax.ShapeDtypeStruct(block, BF16),
            jax.ShapeDtypeStruct(part, F32),
            jax.ShapeDtypeStruct(part, BF16),
            jax.ShapeDtypeStruct(part, BF16),
        )
        scratch.append(pltpu.VMEM((3 * cuts, rows, panels), F32))
    else:
        args.append(earlier)
        specs.append(whole(earlier.shape))
        outs = (jax.ShapeDtypeStruct((steps, panels, rows), BF16),)
    if has_front:
        scratch.append(pltpu.VMEM((3 * cuts, rows, panels), BF16))
    return pl.pallas_call(
        functools.partial(step_body, cuts, pairs, has_front, has_back),
        name="step",
        out_shape=outs,
        grid_spec=pltpu.PrefetchScalarGridSpec(
            num_scalar_prefetch=1,
            grid=(1,),
            in_specs=specs,
            out_specs=tuple(whole(o.shape) for o in outs),
            scratch_shapes=scratch,
        ),
        compiler_params=params(),
        cost_estimate=cost(pairs, 2, rows, panels, 2 * pairs * panels * panels),
    )(loc, *args)


def later_body(cuts, pairs, n, steps, loc, used, *refs):
    extra = steps - 2 - n
    density, own, side, even, odd = refs[:5]
    kerns = refs[5 : 5 + extra]
    ahead, begun, after, sums, near = refs[5 + extra :]
    near[0] = own[...]
    near[1:cuts] = side[...]
    near[cuts : 2 * cuts] = even[...]
    near[2 * cuts :] = odd[...]
    after[...] = ahead[...]
    sums[...] = begun[...]
    rows = density.shape[0]
    for e in range(extra):
        lag = e + 2

        def pair(p, carry, e=e, lag=lag):
            @pl.when(lag <= used[p])
            def _():
                slot = loc[p]
                step = n + lag
                after[step] += dot_nt(near[slot], kerns[e][p, 0])
                sums[slot, pl.ds((step - 1) * rows, rows)] += dot_nn(density[...], kerns[e][p, 0])

            return carry

        lax.fori_loop(0, pairs, pair, 0)


def later_call(n, steps, loc, used, density, near, kern, ahead, begun):
    pairs, _, panels, _ = kern.shape
    rows = density.shape[0]
    extra = steps - 2 - n
    cuts = near[2].shape[0]
    kern_specs = [
        pl.BlockSpec((pairs, 1, panels, panels), lambda *_, e=e: (0, e + 1, 0, 0))
        for e in range(extra)
    ]
    return pl.pallas_call(
        functools.partial(later_body, cuts, pairs, n, steps),
        name="later",
        out_shape=(
            jax.ShapeDtypeStruct(ahead.shape, F32),
            jax.ShapeDtypeStruct(begun.shape, F32),
        ),
        grid_spec=pltpu.PrefetchScalarGridSpec(
            num_scalar_prefetch=2,
            grid=(1,),
            in_specs=[whole(density.shape)]
            + [whole(x.shape) for x in near]
            + kern_specs
            + [whole(ahead.shape), whole(begun.shape)],
            out_specs=(whole(ahead.shape), whole(begun.shape)),
            scratch_shapes=[pltpu.VMEM((3 * cuts, rows, panels), BF16)],
        ),
        compiler_params=params(),
        cost_estimate=cost(pairs, 2 * extra, rows, panels, 2 * extra * pairs * panels * panels),
    )(loc, used, density, *near, *([kern] * extra), ahead, begun)


def gather_near(value):
    cuts = lax.axis_size("cuts")
    side = jnp.stack([cut_exchange(value, j) for j in range(1, cuts)])
    region = jnp.concatenate([value[None], side])
    return value, side, even_exchange(region), odd_exchange(region)


def sum_parts(own, even, odd):
    cuts = lax.axis_size("cuts")
    even, odd = even_exchange(even), odd_exchange(odd)
    total = own + even.astype(F32) + odd.astype(F32)
    moved = total[1:].astype(BF16)
    moved = jnp.stack([cut_exchange(moved[j - 1], j) for j in range(1, cuts)])
    return total[0], moved


def on_device(history, incident, self_inverse, lag_kernels, pair_partner, pair_lags):
    lags, panels, columns = history.shape
    steps = incident.shape[0]
    cuts = lax.axis_size("cuts")
    odd_region = lax.axis_index("region") % 2

    shift = pair_partner // cuts - 1
    side = jnp.where((shift == 1) == (odd_region == 0), 1, 2)
    side = jnp.where(shift == 0, 0, side)
    loc = side * cuts + ((pair_partner % cuts) ^ lax.axis_index("cuts"))

    hist = jnp.swapaxes(history, 1, 2)[::-1]
    incoming = jnp.swapaxes(incident, 1, 2)
    padded = jnp.concatenate([hist, jnp.zeros((steps - 1, columns, panels), BF16)])

    own, even, odd, begun = history_back(loc, pair_lags, padded, lag_kernels, cuts, steps)
    mine, moved = sum_parts(own, even, odd)

    ahead = jnp.zeros((steps, columns, panels), F32)
    at = 0
    for left in range(CHUNKS, 0, -1):
        size = -(-(lags - at) // left)
        times = tuple(range(at - lags, at + size - lags))
        near = gather_near(hist[at : at + size])
        ahead = history_front(loc, pair_lags, near, lag_kernels, ahead, times)
        at += size

    near = None
    densities = []
    for n in range(steps):
        if n + 1 == steps:
            (out,) = step_call(
                n, steps, loc, ahead, mine, moved, incoming, self_inverse, lag_kernels,
                near, None, jnp.stack(densities),
            )
            return out
        density, own, even, odd = step_call(
            n, steps, loc, ahead, mine, moved, incoming, self_inverse, lag_kernels,
            near, begun, None,
        )
        densities.append(density)
        near = gather_near(density)
        mine, moved = sum_parts(own, even, odd)
        if n + 2 < steps:
            ahead, begun = later_call(
                n, steps, loc, pair_lags, density, near, lag_kernels, ahead, begun
            )


def solution(mesh):
    return jax.shard_map(
        on_device,
        mesh=mesh,
        in_specs=(
            P(None, ("region", "cuts"), None),
            P(None, ("region", "cuts"), None),
            P(("region", "cuts"), None),
            P(("region", "cuts"), None, None, None),
            P(("region", "cuts")),
            P(("region", "cuts")),
        ),
        out_specs=P(None, ("region", "cuts"), None),
        check_vma=False,
    )
```

```python
import functools

import jax
import jax.numpy as jnp
from jax import lax
from jax.experimental import pallas as pl
from jax.experimental.pallas import tpu as pltpu
from jax.sharding import PartitionSpec as P


F32 = jnp.float32
BF16 = jnp.bfloat16
IN_VMEM = pl.BlockSpec(memory_space=pltpu.VMEM)
IN_SMEM = pl.BlockSpec(memory_space=pltpu.SMEM)


def dot_nn(a, b):
    return lax.dot_general(a, b, (((1,), (0,)), ((), ())), preferred_element_type=F32)


def dot_nt(a, b):
    return lax.dot_general(a, b, (((1,), (1,)), ((), ())), preferred_element_type=F32)


def even_exchange(value):
    count = lax.axis_size("region")
    return lax.ppermute(value, "region", [(i, i ^ 1) for i in range(count)])


def odd_exchange(value):
    count = lax.axis_size("region")
    route = [(i, (i + 1) % count if i % 2 else (i - 1) % count) for i in range(count)]
    return lax.ppermute(value, "region", route)


def cut_exchange(value, j):
    count = lax.axis_size("cuts")
    return lax.ppermute(value, "cuts", [(i, i ^ j) for i in range(count)])


def cut_pieces(value):
    count = lax.axis_size("cuts")
    if count != 4:
        return [cut_exchange(value, j) for j in range(1, count)]
    inner = [(1, 2), (2, 1)]
    outward = [(1, 0), (2, 3)]
    first = cut_exchange(value, 1)
    across = lax.ppermute(value, "cuts", inner)
    far = lax.ppermute(across, "cuts", outward)
    passed = lax.ppermute(first, "cuts", inner)
    last = lax.ppermute(passed, "cuts", outward)
    return [first, passed + far, across + last]


def call(body, scalars, args, outs, scratch, flops, read, aliases=None, far=(), limit=8):
    return pl.pallas_call(
        body,
        out_shape=outs,
        in_specs=[IN_SMEM] * len(scalars)
        + [pl.BlockSpec(memory_space=pltpu.HBM) if i in far else IN_VMEM for i in range(len(args))],
        input_output_aliases={len(scalars) + i: o for i, o in (aliases or {}).items()},
        out_specs=jax.tree.map(lambda _: IN_VMEM, outs),
        scratch_shapes=scratch,
        compiler_params=pltpu.CompilerParams(vmem_limit_bytes=limit * 1024 * 1024),
        cost_estimate=pl.CostEstimate(
            flops=int(flops) // 1000, bytes_accessed=int(read) // 1000, transcendentals=0
        ),
    )(*scalars, *args)


def gated(kern, lag, last):
    return kern * jnp.where(lag <= last, 1.0, 0.0).astype(BF16)


def lag_chain(dot, block, kern, p, last, steps, add):
    lags = kern.shape[1]
    rows, panels = block.shape[-2:]

    def term(l):
        count = min(steps, l)
        x = block[l - count : l].reshape(count * rows, panels)
        return dot(x, gated(kern[p, l - 1], l, last) if l > 1 else kern[p, l - 1])

    full = None
    for l in range(steps, lags + 1):
        y = term(l)
        full = y if full is None else full + y
    add(0, full)
    for l in range(1, steps):
        add(steps - l, term(l))


def turn_body(value, out):
    for i in range(value.shape[0]):
        out[i] = value[i].T


def enter_body(cuts, codes, history, turned, loc):
    turn_body(history, turned)

    @pl.when(pl.program_id(0) == 0)
    def _():
        odd_region = lax.rem(lax.axis_index("region"), 2)
        own_cut = lax.axis_index("cuts")
        for p in range(codes.shape[0]):
            shift = lax.div(codes[p], cuts) - 1
            side = jnp.where((shift == 1) == (odd_region == 0), 1, 2)
            side = jnp.where(shift == 0, 0, side)
            loc[p] = side * cuts + (lax.rem(codes[p], cuts) ^ own_cut)


def enter(codes, history, cuts):
    count, panels, rows = history.shape
    parts = 2 if count % 2 == 0 else 1
    return pl.pallas_call(
        functools.partial(enter_body, cuts),
        name="enter",
        grid=(parts,),
        in_specs=[
            IN_SMEM,
            pl.BlockSpec((count // parts, panels, rows), lambda i: (i, 0, 0)),
        ],
        out_specs=(pl.BlockSpec((count // parts, rows, panels), lambda i: (i, 0, 0)), IN_SMEM),
        out_shape=(
            jax.ShapeDtypeStruct((count, rows, panels), history.dtype),
            jax.ShapeDtypeStruct(codes.shape, codes.dtype),
        ),
        compiler_params=pltpu.CompilerParams(vmem_limit_bytes=8 * 1024 * 1024),
        cost_estimate=pl.CostEstimate(flops=0, bytes_accessed=4096, transcendentals=0),
    )(codes, history)


def history_back_body(
    steps, cuts, loc, used, hist, given, stored, incoming, own, even, odd, *sums
):
    rows = hist.shape[1]
    begun, (first, kern, done) = sums[:-3], sums[-3:]
    heaps = list(begun[::-1]) + [first]
    copies = [
        pltpu.make_async_copy(stored.at[p], kern.at[p], done.at[p])
        for p in range(kern.shape[0])
    ]
    for copy in copies:
        copy.start()
    for heap in heaps:
        heap[...] = jnp.zeros_like(heap)
    turn_body(given, incoming)

    def pair(p, carry):
        slot = loc[p]
        pltpu.make_async_copy(stored.at[p], kern.at[p], done.at[p]).wait()

        def add(low, y):
            for i in range(low, steps):
                heaps[i][slot] += y[(i - low) * rows : (i - low + 1) * rows]

        lag_chain(dot_nn, hist, kern, p, used[p], steps, add)
        return carry

    lax.fori_loop(0, kern.shape[0], pair, 0)
    own[...] = first[:cuts]
    even[...] = first[cuts : 2 * cuts].astype(BF16)
    odd[...] = first[2 * cuts :].astype(BF16)


def history_back(loc, used, hist, incident, kern, cuts):
    steps = incident.shape[0]
    pairs, lags, panels, _ = kern.shape
    rows = hist.shape[1]
    part = (cuts, rows, panels)
    heap = (3 * cuts, rows, panels)
    outs = (
        jax.ShapeDtypeStruct((steps, rows, panels), BF16),
        jax.ShapeDtypeStruct(part, F32),
        jax.ShapeDtypeStruct(part, BF16),
        jax.ShapeDtypeStruct(part, BF16),
    ) + (jax.ShapeDtypeStruct(heap, F32),) * (steps - 1)
    return call(
        functools.partial(history_back_body, steps, cuts),
        (loc, used),
        (hist, incident, kern),
        outs,
        [
            pltpu.VMEM(heap, F32),
            pltpu.VMEM(kern.shape, BF16),
            pltpu.SemaphoreType.DMA((pairs,)),
        ],
        2 * pairs * lags * steps * rows * panels * panels,
        2 * kern.size,
        far=(2,),
        limit=36,
    )


def history_front_body(slots, steps, has_before, loc, used, kern, *refs):
    blocks = refs[: len(slots)]
    refs = refs[len(slots) :]
    after, near = refs[-2:]
    rows = near.shape[2]
    for i, block in enumerate(blocks):
        near[i] = block[...]
    after[...] = refs[0][...] if has_before else jnp.zeros_like(after)

    def pair(p, carry):
        slot = loc[p]
        at = jnp.int32(-1)
        for i, s in enumerate(slots):
            at = jnp.where(slot == s, i, at)

        @pl.when(at >= 0)
        def _():
            def add(low, y):
                after[low:] += y.reshape(steps - low, rows, y.shape[-1])

            lag_chain(dot_nt, near.at[at], kern, p, used[p], steps, add)

        return carry

    lax.fori_loop(0, kern.shape[0], pair, 0)


def history_front(loc, used, kern, near, before, steps):
    pairs, lags, panels, _ = kern.shape
    slots = tuple(near)
    blocks = [near[s] for s in slots]
    rows = blocks[0].shape[1]
    share = len(slots) / 12
    return call(
        functools.partial(history_front_body, slots, steps, before is not None),
        (loc, used),
        [kern] + blocks + ([] if before is None else [before]),
        jax.ShapeDtypeStruct((steps, rows, panels), F32),
        [pltpu.VMEM((len(slots), lags, rows, panels), BF16)],
        share * 2 * pairs * lags * steps * rows * panels * panels,
        share * 2 * kern.size,
    )


def fill_near(near, own, side, even, odd):
    cuts = even.shape[0]
    near[0] = own[...]
    near[1:cuts] = side[...]
    near[cuts : 2 * cuts] = even[...]
    near[2 * cuts :] = odd[...]


def step_body(n, at, cuts, pairs, has_front, has_back, loc, *refs):
    refs = list(refs)
    ahead, mine, moved, incoming, inverse, kern = refs[:6]
    refs = refs[6:]
    total = ahead[at] + mine[...]
    for j in range(cuts - 1):
        total = total + moved[j].astype(F32)
    if has_front:
        near = refs[-1]
        fill_near(near, *refs[:4])
        refs = refs[4:]
        for p in range(pairs):
            total = total + dot_nt(near[loc[p]], kern[p, 0])
    excess = (incoming[n].astype(F32) - total).astype(BF16)
    density = dot_nt(excess, inverse[...]).astype(BF16)
    if has_back:
        _, out, out_own, out_even, out_odd, sums = refs[:6]
        out[...] = density
        for p in range(pairs):
            sums[loc[p]] += dot_nn(density, kern[p, 0])
        out_own[...] = sums[:cuts]
        out_even[...] = sums[cuts : 2 * cuts].astype(BF16)
        out_odd[...] = sums[2 * cuts :].astype(BF16)
    else:
        earlier, out = refs[: n], refs[n]
        for m in range(n):
            out[m] = earlier[m][...].astype(F32).T.astype(BF16)
        out[n] = density.astype(F32).T.astype(BF16)


def step_call(n, steps, loc, ahead, mine, moved, incoming, inverse, kern, near, begun, earlier):
    pairs, _, panels, _ = kern.shape
    cuts = moved.shape[0] + 1
    rows = mine.shape[0]
    has_front = near is not None
    has_back = n + 1 < steps
    part = (cuts, rows, panels)
    heap = (3 * cuts, rows, panels)
    ahead, at = ahead
    args = [ahead, mine, moved, incoming, inverse, kern]
    scratch = []
    aliases = {}
    if has_front:
        args += list(near)
    if has_back:
        args.append(begun)
        outs = (
            jax.ShapeDtypeStruct((rows, panels), BF16),
            jax.ShapeDtypeStruct(part, F32),
            jax.ShapeDtypeStruct(part, BF16),
            jax.ShapeDtypeStruct(part, BF16),
            jax.ShapeDtypeStruct(heap, F32),
        )
        aliases[len(args) - 1] = 4
    else:
        args += earlier
        outs = jax.ShapeDtypeStruct((steps, panels, rows), BF16)
    if has_front:
        scratch.append(pltpu.VMEM(heap, BF16))
    return call(
        functools.partial(step_body, n, at, cuts, pairs, has_front, has_back),
        (loc,),
        args,
        outs,
        scratch,
        4 * pairs * rows * panels * panels,
        2 * pairs * panels * panels,
        aliases=aliases,
    )


def later_body(back, front, loc, used, kern, *refs):
    refs = list(refs)
    has_near = bool(front)
    near = refs.pop() if has_near else None
    news = refs[len(refs) - len(back) - len(front) :]
    density = refs.pop(0) if back else None
    if has_near:
        fill_near(near, *refs[:4])
        refs = refs[4:]
    rows = [refs[len(back) + i][at] for i, (_, at) in enumerate(front)]
    for p in range(kern.shape[0]):
        slot = loc[p]
        last = used[p]
        for i, lag in enumerate(back):
            news[i][slot] += dot_nn(density[...], gated(kern[p, lag - 1], lag, last))
        for i, (lag, _) in enumerate(front):
            rows[i] += dot_nt(near[slot], gated(kern[p, lag - 1], lag, last))
    for i in range(len(front)):
        news[len(back) + i][0] = rows[i]


def later_call(loc, used, kern, cuts, density, back, near, front):
    pairs, _, panels, _ = kern.shape
    args = [kern]
    scratch = []
    if back:
        args.append(density)
    if front:
        args += list(near)
        scratch.append(pltpu.VMEM((3 * cuts,) + near[0].shape, BF16))
    args += [sums for _, sums in back] + [sums for _, (sums, _) in front]
    rows = (density if back else near[0]).shape[0]
    outs = [jax.ShapeDtypeStruct(sums.shape, F32) for _, sums in back]
    outs += [jax.ShapeDtypeStruct((1, rows, panels), F32) for _ in front]
    terms = len(back) + len(front)
    return call(
        functools.partial(
            later_body, [lag for lag, _ in back], [(lag, at) for lag, (_, at) in front]
        ),
        (loc, used),
        args,
        tuple(outs),
        scratch,
        2 * terms * pairs * rows * panels * panels,
        2 * terms * pairs * panels * panels,
        aliases={len(args) - len(back) - len(front) + i: i for i in range(len(back))},
    )


def gather_near(value):
    cuts = lax.axis_size("cuts")
    side = []
    for j in range(1, cuts):
        side.append(cut_exchange(value, j))
    side = jnp.stack(side)
    region = jnp.concatenate([value[None], side])
    odd = odd_exchange(region)
    even = even_exchange(region)
    return value, side, even, odd


def sum_parts(own, even, odd):
    cuts = lax.axis_size("cuts")
    odd = odd_exchange(odd)
    even = even_exchange(even)
    total = own + even.astype(F32) + odd.astype(F32)
    part = total[1:].astype(BF16)
    moved = []
    for j in range(1, cuts):
        moved.append(cut_exchange(part[j - 1], j))
    return total[0], jnp.stack(moved)


def every_step(history, incident, self_inverse, lag_kernels, pair_partner, pair_lags):
    steps = incident.shape[0]
    cuts = lax.axis_size("cuts")
    hist, loc = enter(pair_partner, history, cuts)
    incoming, own, even, odd, *begun = history_back(
        loc, pair_lags, hist, incident, lag_kernels, cuts
    )
    begun = dict(enumerate(begun, 1))
    mine, moved = sum_parts(own, even, odd)

    pieces = [hist] + cut_pieces(hist)
    evens, odds = [], []
    for piece in pieces:
        odds.append(odd_exchange(piece))
        evens.append(even_exchange(piece))
    sums = None
    for group in range(1, cuts + 1):
        near = {}
        if group < cuts:
            own_slots = range(group + 1) if group == 1 else [group]
            near.update({j: pieces[j] for j in own_slots})
        near[cuts + group - 1] = evens[group - 1]
        near[2 * cuts + group - 1] = odds[group - 1]
        sums = history_front(loc, pair_lags, lag_kernels, near, sums, steps)
    ahead = {n: (sums, steps - 1 - n) for n in range(steps)}

    near = None
    densities = []
    for n in range(steps - 1):
        density, own, even, odd, _ = step_call(
            n, steps, loc, ahead[n], mine, moved, incoming, self_inverse, lag_kernels,
            near, begun.get(n + 1), None,
        )
        densities.append(density)
        before, near = near, gather_near(density)
        mine, moved = sum_parts(own, even, odd)
        back = [(m - n, begun[m]) for m in range(n + 2, steps)]
        front = [(m - n + 1, ahead[m]) for m in range(n + 1, steps)] if n else []
        if back or front:
            news = later_call(loc, pair_lags, lag_kernels, cuts, density, back, before, front)
            for i, m in enumerate(range(n + 2, steps)):
                begun[m] = news[i]
            if n:
                for i, m in enumerate(range(n + 1, steps)):
                    ahead[m] = (news[len(back) + i], 0)
    return step_call(
        steps - 1, steps, loc, ahead[steps - 1], mine, moved, incoming, self_inverse,
        lag_kernels, near, None, densities,
    )


def solution(mesh):
    return jax.shard_map(
        every_step,
        mesh=mesh,
        in_specs=(
            P(None, ("region", "cuts"), None),
            P(None, ("region", "cuts"), None),
            P(("region", "cuts"), None),
            P(("region", "cuts"), None, None, None),
            P(("region", "cuts")),
            P(("region", "cuts")),
        ),
        out_specs=P(None, ("region", "cuts"), None),
        check_vma=False,
    )
```

```python
import functools

import jax
import jax.numpy as jnp
from jax import lax
from jax.experimental import pallas as pl
from jax.experimental.pallas import tpu as pltpu
from jax.sharding import PartitionSpec as P


F32 = jnp.float32
BF16 = jnp.bfloat16
IN_VMEM = pl.BlockSpec(memory_space=pltpu.VMEM)
IN_SMEM = pl.BlockSpec(memory_space=pltpu.SMEM)


def dot_nn(a, b):
    return lax.dot_general(a, b, (((1,), (0,)), ((), ())), preferred_element_type=F32)


def dot_nt(a, b):
    return lax.dot_general(a, b, (((1,), (1,)), ((), ())), preferred_element_type=F32)


def even_exchange(value):
    count = lax.axis_size("region")
    return lax.ppermute(value, "region", [(i, i ^ 1) for i in range(count)])


def odd_exchange(value):
    count = lax.axis_size("region")
    route = [(i, (i + 1) % count if i % 2 else (i - 1) % count) for i in range(count)]
    return lax.ppermute(value, "region", route)


def cut_exchange(value, j):
    count = lax.axis_size("cuts")
    return lax.ppermute(value, "cuts", [(i, i ^ j) for i in range(count)])


def cut_pieces(value):
    count = lax.axis_size("cuts")
    if count != 4:
        return {j: cut_exchange(value, j) for j in range(1, count)}
    inner = [(1, 2), (2, 1)]
    outward = [(1, 0), (2, 3)]
    first = cut_exchange(value, 1)
    across = lax.ppermute(value, "cuts", inner)
    far = lax.ppermute(across, "cuts", outward)
    passed = lax.ppermute(first, "cuts", inner)
    ends = lax.ppermute(value, "cuts", [(0, 3), (3, 0)])
    return {1: first, 3: across + ends, 2: passed + far}


def call(body, scalars, args, outs, scratch, flops, read, aliases=None, far=(), limit=8):
    return pl.pallas_call(
        body,
        out_shape=outs,
        in_specs=[IN_SMEM] * len(scalars)
        + [pl.BlockSpec(memory_space=pltpu.HBM) if i in far else IN_VMEM for i in range(len(args))],
        input_output_aliases={len(scalars) + i: o for i, o in (aliases or {}).items()},
        out_specs=jax.tree.map(lambda _: IN_VMEM, outs),
        scratch_shapes=scratch,
        compiler_params=pltpu.CompilerParams(vmem_limit_bytes=limit * 1024 * 1024),
        cost_estimate=pl.CostEstimate(
            flops=int(flops) // 1000, bytes_accessed=int(read) // 1000, transcendentals=0
        ),
    )(*scalars, *args)


def gated(kern, lag, last):
    return kern * jnp.where(lag <= last, 1.0, 0.0).astype(BF16)


def lag_chain(dot, block, kern, p, last, low, high, add):
    lags = kern.shape[1]
    rows, panels = block.shape[-2:]
    full = None
    for l in range(lags, low, -1):
        top = min(high, l)
        x = block[l - top : l - low].reshape((top - low) * rows, panels)
        y = dot(x, gated(kern[p, l - 1], l, last) if l > 1 else kern[p, l - 1])
        if top == high:
            full = y if full is None else full + y
            if l == max(high, low + 1):
                add(0, full)
        else:
            add(high - top, y)


def turn_body(value, out):
    for i in range(value.shape[0]):
        out[i] = value[i].T


def turned(value):
    count, panels, rows = value.shape
    return call(
        turn_body, (), (value,),
        jax.ShapeDtypeStruct((count, rows, panels), value.dtype), [], 0, 4 * value.size,
    )


def enter_body(cuts, codes, lags, history, out, loc, used):
    turn_body(history, out)

    @pl.when(pl.program_id(0) == 0)
    def _():
        odd_region = lax.rem(lax.axis_index("region"), 2)
        own_cut = lax.axis_index("cuts")
        for p in range(codes.shape[0]):
            used[p] = lags[p]
            shift = lax.div(codes[p], cuts) - 1
            side = jnp.where((shift == 1) == (odd_region == 0), 1, 2)
            side = jnp.where(shift == 0, 0, side)
            loc[p] = side * cuts + (lax.rem(codes[p], cuts) ^ own_cut)


def enter(codes, lags, history, cuts):
    count, panels, rows = history.shape
    parts = 2 if count % 2 == 0 else 1
    return pl.pallas_call(
        functools.partial(enter_body, cuts),
        name="enter",
        grid=(parts,),
        in_specs=[
            IN_SMEM,
            IN_SMEM,
            pl.BlockSpec((count // parts, panels, rows), lambda i: (i, 0, 0)),
        ],
        out_specs=(pl.BlockSpec((count // parts, rows, panels), lambda i: (i, 0, 0)), IN_SMEM, IN_SMEM),
        out_shape=(
            jax.ShapeDtypeStruct((count, rows, panels), history.dtype),
            jax.ShapeDtypeStruct(codes.shape, codes.dtype),
            jax.ShapeDtypeStruct(lags.shape, lags.dtype),
        ),
        compiler_params=pltpu.CompilerParams(vmem_limit_bytes=8 * 1024 * 1024),
        cost_estimate=pl.CostEstimate(flops=0, bytes_accessed=4096, transcendentals=0),
    )(codes, lags, history)


def history_back_body(steps, cuts, first, low, high, loc, used, hist, kern, *refs):
    rows = hist.shape[1]
    if first:
        heaps, (held, done) = refs[:steps], refs[steps:]
        for p in range(low, high):
            pltpu.make_async_copy(kern.at[p], held.at[p - low], done.at[p - low]).start()
        for heap in heaps:
            heap[...] = jnp.zeros_like(heap)
    else:
        heaps, (own, even, odd) = refs[steps : 2 * steps], refs[2 * steps :]
        held = kern

    def pair(q, carry):
        p = low + q
        slot = loc[p]
        if first:
            pltpu.make_async_copy(kern.at[p], held.at[q], done.at[q]).wait()

        def add(at, y):
            for i in range(at, steps):
                heaps[i][slot] += y[(i - at) * rows : (i - at + 1) * rows]

        lag_chain(dot_nn, hist, held, q if first else p, used[p], 0, steps, add)
        return carry

    lax.fori_loop(0, high - low, pair, 0)
    if not first:
        total = heaps[steps - 1]
        own[...] = total[:cuts]
        even[...] = total[cuts : 2 * cuts].astype(BF16)
        odd[...] = total[2 * cuts :].astype(BF16)


def history_back(loc, used, hist, kern, cuts, steps, low, high, heaps):
    _, lags, panels, _ = kern.shape
    rows = hist.shape[1]
    first = heaps is None
    part = (cuts, rows, panels)
    heap = jax.ShapeDtypeStruct((3 * cuts, rows, panels), F32)
    outs = (heap,) * steps
    if not first:
        outs += (
            jax.ShapeDtypeStruct(part, F32),
            jax.ShapeDtypeStruct(part, BF16),
            jax.ShapeDtypeStruct(part, BF16),
        )
    count = high - low
    return call(
        functools.partial(history_back_body, steps, cuts, first, low, high),
        (loc, used),
        [hist, kern] + ([] if first else list(heaps)),
        outs,
        [pltpu.VMEM((count,) + kern.shape[1:], BF16), pltpu.SemaphoreType.DMA((count,))]
        if first
        else [],
        2 * count * lags * steps * rows * panels * panels,
        2 * kern.size,
        aliases=None if first else {2 + i: i for i in range(steps)},
        far=(1,) if first else (),
        limit=40 if first else 8,
    )


def history_front_body(slots, low, high, has_before, loc, used, kern, *refs):
    blocks = refs[: len(slots)]
    refs = refs[len(slots) :]
    after, near = refs[-2:]
    rows = near.shape[2]
    for i, block in enumerate(blocks):
        near[i] = block[...]
    after[...] = refs[0][: high - low] if has_before else jnp.zeros_like(after)

    def pair(p, carry):
        slot = loc[p]
        at = jnp.int32(-1)
        for i, s in enumerate(slots):
            at = jnp.where(slot == s, i, at)

        @pl.when(at >= 0)
        def _():
            def add(i, y):
                after[i:] += y.reshape(high - low - i, rows, y.shape[-1])

            lag_chain(dot_nt, near.at[at], kern, p, used[p], low, high, add)

        return carry

    lax.fori_loop(0, kern.shape[0], pair, 0)


def history_front(loc, used, kern, near, before, low, high):
    pairs, lags, panels, _ = kern.shape
    slots = tuple(near)
    blocks = [near[s] for s in slots]
    rows = blocks[0].shape[1]
    share = len(slots) / 12
    return call(
        functools.partial(history_front_body, slots, low, high, before is not None),
        (loc, used),
        [kern] + blocks + ([] if before is None else [before]),
        jax.ShapeDtypeStruct((high - low, rows, panels), F32),
        [pltpu.VMEM((len(slots), lags, rows, panels), BF16)],
        share * 2 * pairs * lags * (high - low) * rows * panels * panels,
        share * 2 * kern.size,
    )


def fill_near(near, own, side, even, odd):
    cuts = even.shape[0]
    near[0] = own[...]
    near[1:cuts] = side[...]
    near[cuts : 2 * cuts] = even[...]
    near[2 * cuts :] = odd[...]


def step_body(n, at, cuts, pairs, has_front, has_back, final, loc, used, *refs):
    refs = list(refs)
    ahead, mine, incoming, inverse, kern = refs[:5]
    moved, refs = refs[5 : 4 + cuts], refs[4 + cuts :]
    total = ahead[at] + mine[...]
    for part in moved:
        total = total + part[...].astype(F32)
    if has_front:
        near = refs[-1]
        fill_near(near, *refs[:4])
        refs = refs[4:]
        for p in range(pairs):
            total = total + dot_nt(near[loc[p]], kern[p, 0])
    if final:
        blocks, rest = refs[: len(final)], refs[-1]
        refs = refs[len(final) :]
        rest[...] = total
        for block, slot in zip(blocks, final):

            def pair(p, carry, block=block, slot=slot):
                @pl.when(loc[p] == slot)
                def _():
                    def add(_, y):
                        rest[...] += y

                    lag_chain(dot_nt, block, kern, p, used[p], 0, 1, add)

                return carry

            lax.fori_loop(0, pairs, pair, 0)
        total = rest[...]
    excess = (incoming[n].astype(F32) - total).astype(BF16)
    density = dot_nt(excess, inverse[...]).astype(BF16)
    if has_back:
        _, out, out_own, out_even, out_odd, sums = refs[:6]
        out[...] = density
        for p in range(pairs):
            sums[loc[p]] += dot_nn(density, kern[p, 0])
        out_own[...] = sums[:cuts]
        out_even[...] = sums[cuts : 2 * cuts].astype(BF16)
        out_odd[...] = sums[2 * cuts :].astype(BF16)
    else:
        earlier, out = refs[: n], refs[n]
        for m in range(n):
            out[m] = earlier[m][...].astype(F32).T.astype(BF16)
        out[n] = density.astype(F32).T.astype(BF16)


def step_call(
    n, steps, loc, used, ahead, mine, moved, incoming, inverse, kern, near, begun, earlier, final
):
    pairs, _, panels, _ = kern.shape
    cuts = len(moved) + 1
    rows = mine.shape[0]
    has_front = near is not None
    has_back = n + 1 < steps
    part = (cuts, rows, panels)
    heap = (3 * cuts, rows, panels)
    ahead, at = ahead
    args = [ahead, mine, incoming, inverse, kern] + moved
    scratch = []
    aliases = {}
    if has_front:
        args += list(near)
    args += list(final.values())
    if has_back:
        args.append(begun)
        outs = (
            jax.ShapeDtypeStruct((rows, panels), BF16),
            jax.ShapeDtypeStruct(part, F32),
            jax.ShapeDtypeStruct(part, BF16),
            jax.ShapeDtypeStruct(part, BF16),
            jax.ShapeDtypeStruct(heap, F32),
        )
        aliases[len(args) - 1] = 4
    else:
        args += earlier
        outs = jax.ShapeDtypeStruct((steps, panels, rows), BF16)
    if has_front:
        scratch.append(pltpu.VMEM(heap, BF16))
    if final:
        scratch.append(pltpu.VMEM((rows, panels), F32))
    return call(
        functools.partial(step_body, n, at, cuts, pairs, has_front, has_back, tuple(final)),
        (loc, used),
        args,
        outs,
        scratch,
        4 * pairs * rows * panels * panels,
        2 * pairs * panels * panels,
        aliases=aliases,
    )


def later_body(back, front, loc, used, kern, *refs):
    refs = list(refs)
    has_near = bool(front)
    near = refs.pop() if has_near else None
    news = refs[len(refs) - len(back) - len(front) :]
    density = refs.pop(0) if back else None
    if has_near:
        fill_near(near, *refs[:4])
        refs = refs[4:]
    rows = [refs[len(back) + i][at] for i, (_, at) in enumerate(front)]
    for p in range(kern.shape[0]):
        slot = loc[p]
        last = used[p]
        for i, lag in enumerate(back):
            news[i][slot] += dot_nn(density[...], gated(kern[p, lag - 1], lag, last))
        for i, (lag, _) in enumerate(front):
            rows[i] += dot_nt(near[slot], gated(kern[p, lag - 1], lag, last))
    for i in range(len(front)):
        news[len(back) + i][0] = rows[i]


def later_call(loc, used, kern, cuts, density, back, near, front):
    pairs, _, panels, _ = kern.shape
    args = [kern]
    scratch = []
    if back:
        args.append(density)
    if front:
        args += list(near)
        scratch.append(pltpu.VMEM((3 * cuts,) + near[0].shape, BF16))
    args += [sums for _, sums in back] + [sums for _, (sums, _) in front]
    rows = (density if back else near[0]).shape[0]
    outs = [jax.ShapeDtypeStruct(sums.shape, F32) for _, sums in back]
    outs += [jax.ShapeDtypeStruct((1, rows, panels), F32) for _ in front]
    terms = len(back) + len(front)
    return call(
        functools.partial(
            later_body, [lag for lag, _ in back], [(lag, at) for lag, (_, at) in front]
        ),
        (loc, used),
        args,
        tuple(outs),
        scratch,
        2 * terms * pairs * rows * panels * panels,
        2 * terms * pairs * panels * panels,
        aliases={len(args) - len(back) - len(front) + i: i for i in range(len(back))},
    )


def gather_near(value):
    cuts = lax.axis_size("cuts")
    side = []
    for j in range(1, cuts):
        side.append(cut_exchange(value, j))
    side = jnp.stack(side)
    region = jnp.concatenate([value[None], side])
    odd = odd_exchange(region)
    even = even_exchange(region)
    return value, side, even, odd


def total_body(own, even, odd, mine, *parts):
    for j in range(own.shape[0]):
        total = own[j] + even[j].astype(F32) + odd[j].astype(F32)
        if j:
            parts[j - 1][...] = total.astype(BF16)
        else:
            mine[...] = total


def sum_parts(own, even, odd):
    cuts = lax.axis_size("cuts")
    odd = odd_exchange(odd)
    even = even_exchange(even)
    mine, *part = call(
        total_body, (), (own, even, odd),
        (jax.ShapeDtypeStruct(own.shape[1:], F32),)
        + (jax.ShapeDtypeStruct(own.shape[1:], BF16),) * (cuts - 1),
        [], 2 * own.size, 8 * own.size,
    )
    moved = []
    for j in range(1, cuts):
        moved.append(cut_exchange(part[j - 1], j))
    return mine, moved


def every_step(history, incident, self_inverse, lag_kernels, pair_partner, pair_lags):
    steps = incident.shape[0]
    cuts = lax.axis_size("cuts")
    hist, loc, used = enter(pair_partner, pair_lags, history, cuts)
    incoming = turned(incident)

    half = pair_lags.shape[0] // 2
    heaps = history_back(loc, used, hist, lag_kernels, cuts, steps, 0, half, None)
    *heaps, own, even, odd = history_back(
        loc, used, hist, lag_kernels, cuts, steps, half, pair_lags.shape[0], heaps
    )
    begun = {steps - 1 - i: heap for i, heap in enumerate(heaps)}
    mine, moved = sum_parts(own, even, odd)

    pieces = {0: hist, **cut_pieces(hist)}
    blocks = {}
    for j, piece in pieces.items():
        odd = odd_exchange(piece)
        even = even_exchange(piece)
        blocks.update({j: piece, cuts + j: even, 2 * cuts + j: odd})
    *_, j_late, j_final = pieces
    final = {slot: blocks.pop(slot) for slot in range(j_final, 3 * cuts, cuts)}
    late = {slot: blocks.pop(slot) for slot in (cuts + j_late, 2 * cuts + j_late)}
    sums = history_front(loc, used, lag_kernels, blocks, None, 0, steps)
    sums = history_front(loc, used, lag_kernels, late, sums, 0, steps)
    ahead = {n: (sums, steps - 1 - n) for n in range(steps)}

    near = None
    densities = []
    for n in range(steps - 1):
        density, own, even, odd, _ = step_call(
            n, steps, loc, used, ahead[n], mine, moved, incoming, self_inverse, lag_kernels,
            near, begun.get(n + 1), None, {} if n else final,
        )
        densities.append(density)
        before, near = near, gather_near(density)
        mine, moved = sum_parts(own, even, odd)
        if n == 0:
            sums = history_front(loc, used, lag_kernels, final, sums, 1, steps)
            ahead = {m: (sums, steps - 1 - m) for m in range(1, steps)}
        back = [(m - n, begun[m]) for m in range(n + 2, steps)]
        front = [(m - n + 1, ahead[m]) for m in range(n + 1, steps)] if n else []
        if back or front:
            news = later_call(loc, used, lag_kernels, cuts, density, back, before, front)
            for i, m in enumerate(range(n + 2, steps)):
                begun[m] = news[i]
            if n:
                for i, m in enumerate(range(n + 1, steps)):
                    ahead[m] = (news[len(back) + i], 0)
    return step_call(
        steps - 1, steps, loc, used, ahead[steps - 1], mine, moved, incoming, self_inverse,
        lag_kernels, near, None, densities, {},
    )


def solution(mesh):
    return jax.shard_map(
        every_step,
        mesh=mesh,
        in_specs=(
            P(None, ("region", "cuts"), None),
            P(None, ("region", "cuts"), None),
            P(("region", "cuts"), None),
            P(("region", "cuts"), None, None, None),
            P(("region", "cuts")),
            P(("region", "cuts")),
        ),
        out_specs=P(None, ("region", "cuts"), None),
        check_vma=False,
    )
```

```python
import functools

import jax
import jax.numpy as jnp
from jax import lax
from jax.experimental import pallas as pl
from jax.experimental.pallas import tpu as pltpu
from jax.sharding import PartitionSpec as P


F32 = jnp.float32
BF16 = jnp.bfloat16
IN_VMEM = pl.BlockSpec(memory_space=pltpu.VMEM)
IN_SMEM = pl.BlockSpec(memory_space=pltpu.SMEM)


def dot_nn(a, b):
    return lax.dot_general(a, b, (((1,), (0,)), ((), ())), preferred_element_type=F32)


def dot_nt(a, b):
    return lax.dot_general(a, b, (((1,), (1,)), ((), ())), preferred_element_type=F32)


def even_exchange(value):
    count = lax.axis_size("region")
    return lax.ppermute(value, "region", [(i, i ^ 1) for i in range(count)])


def odd_exchange(value):
    count = lax.axis_size("region")
    route = [(i, (i + 1) % count if i % 2 else (i - 1) % count) for i in range(count)]
    return lax.ppermute(value, "region", route)


def cut_exchange(value, j):
    count = lax.axis_size("cuts")
    return lax.ppermute(value, "cuts", [(i, i ^ j) for i in range(count)])


def cut_pieces(value):
    count = lax.axis_size("cuts")
    if count != 4:
        return {j: cut_exchange(value, j) for j in range(1, count)}
    inner = [(1, 2), (2, 1)]
    outward = [(1, 0), (2, 3)]
    first = cut_exchange(value, 1)
    across = lax.ppermute(value, "cuts", inner)
    far = lax.ppermute(across, "cuts", outward)
    passed = lax.ppermute(first, "cuts", inner)
    ends = lax.ppermute(value, "cuts", [(0, 3), (3, 0)])
    return {1: first, 3: across + ends, 2: passed + far}


def call(body, scalars, args, outs, scratch, flops, read, aliases=None, far=(), limit=8):
    return pl.pallas_call(
        body,
        out_shape=outs,
        in_specs=[IN_SMEM] * len(scalars)
        + [pl.BlockSpec(memory_space=pltpu.HBM) if i in far else IN_VMEM for i in range(len(args))],
        input_output_aliases={len(scalars) + i: o for i, o in (aliases or {}).items()},
        out_specs=jax.tree.map(lambda _: IN_VMEM, outs),
        scratch_shapes=scratch,
        compiler_params=pltpu.CompilerParams(vmem_limit_bytes=limit * 1024 * 1024),
        cost_estimate=pl.CostEstimate(
            flops=int(flops) // 1000, bytes_accessed=int(read) // 1000, transcendentals=0
        ),
    )(*scalars, *args)


def gated(kern, lag, last):
    return kern * jnp.where(lag <= last, 1.0, 0.0).astype(BF16)


def lag_chain(dot, block, kern, p, last, low, high, add):
    lags = kern.shape[1]
    rows, panels = block.shape[-2:]
    full = None
    for l in range(lags, low, -1):
        top = min(high, l)
        x = block[l - top : l - low].reshape((top - low) * rows, panels)
        y = dot(x, gated(kern[p, l - 1], l, last) if l > 1 else kern[p, l - 1])
        if top == high:
            full = y if full is None else full + y
            if l == max(high, low + 1):
                add(0, full)
        else:
            add(high - top, y)


def turn_body(value, out):
    for i in range(value.shape[0]):
        out[i] = value[i].T


def turned(value):
    count, panels, rows = value.shape
    return call(
        turn_body, (), (value,),
        jax.ShapeDtypeStruct((count, rows, panels), value.dtype), [], 0, 4 * value.size,
    )


def enter_body(cuts, codes, lags, history, out, loc, used):
    turn_body(history, out)
    odd_region = lax.rem(lax.axis_index("region"), 2)
    own_cut = lax.axis_index("cuts")
    for p in range(codes.shape[0]):
        used[p] = lags[p]
        shift = lax.div(codes[p], cuts) - 1
        side = jnp.where((shift == 1) == (odd_region == 0), 1, 2)
        side = jnp.where(shift == 0, 0, side)
        loc[p] = side * cuts + (lax.rem(codes[p], cuts) ^ own_cut)


def enter(codes, lags, history, cuts):
    count, panels, rows = history.shape
    return pl.pallas_call(
        functools.partial(enter_body, cuts),
        name="enter",
        in_specs=[IN_SMEM, IN_SMEM, IN_VMEM],
        out_specs=(IN_VMEM, IN_SMEM, IN_SMEM),
        out_shape=(
            jax.ShapeDtypeStruct((count, rows, panels), history.dtype),
            jax.ShapeDtypeStruct(codes.shape, codes.dtype),
            jax.ShapeDtypeStruct(lags.shape, lags.dtype),
        ),
        compiler_params=pltpu.CompilerParams(vmem_limit_bytes=8 * 1024 * 1024),
    )(codes, lags, history)


def history_back_body(steps, cuts, first, low, high, loc, used, hist, kern, *refs):
    rows = hist.shape[1]
    if first:
        heaps, (held, done) = refs[:steps], refs[steps:]
        for p in range(low, high):
            pltpu.make_async_copy(kern.at[p], held.at[p - low], done.at[p - low]).start()
        for heap in heaps:
            heap[...] = jnp.zeros_like(heap)
    else:
        heaps, (own, even, odd) = refs[steps : 2 * steps], refs[2 * steps :]
        held = kern

    def pair(q, carry):
        p = low + q
        slot = loc[p]
        if first:
            pltpu.make_async_copy(kern.at[p], held.at[q], done.at[q]).wait()

        def add(at, y):
            for i in range(at, steps):
                heaps[i][slot] += y[(i - at) * rows : (i - at + 1) * rows]

        lag_chain(dot_nn, hist, held, q if first else p, used[p], 0, steps, add)
        return carry

    lax.fori_loop(0, high - low, pair, 0)
    if not first:
        total = heaps[steps - 1]
        own[...] = total[:cuts]
        even[...] = total[cuts : 2 * cuts].astype(BF16)
        odd[...] = total[2 * cuts :].astype(BF16)


def history_back(loc, used, hist, kern, cuts, steps, low, high, heaps):
    _, lags, panels, _ = kern.shape
    rows = hist.shape[1]
    first = heaps is None
    part = (cuts, rows, panels)
    heap = jax.ShapeDtypeStruct((3 * cuts, rows, panels), F32)
    outs = (heap,) * steps
    if not first:
        outs += (
            jax.ShapeDtypeStruct(part, F32),
            jax.ShapeDtypeStruct(part, BF16),
            jax.ShapeDtypeStruct(part, BF16),
        )
    count = high - low
    return call(
        functools.partial(history_back_body, steps, cuts, first, low, high),
        (loc, used),
        [hist, kern] + ([] if first else list(heaps)),
        outs,
        [pltpu.VMEM((count,) + kern.shape[1:], BF16), pltpu.SemaphoreType.DMA((count,))]
        if first
        else [],
        2 * count * lags * steps * rows * panels * panels,
        2 * kern.size,
        aliases=None if first else {2 + i: i for i in range(steps)},
        far=(1,) if first else (),
        limit=40 if first else 8,
    )


def history_front_body(slots, low, high, has_before, loc, used, kern, *refs):
    blocks = refs[: len(slots)]
    refs = refs[len(slots) :]
    after, near = refs[-2:]
    rows = near.shape[2]
    for i, block in enumerate(blocks):
        near[i] = block[...]
    after[...] = refs[0][: high - low] if has_before else jnp.zeros_like(after)

    def pair(p, carry):
        slot = loc[p]
        at = jnp.int32(-1)
        for i, s in enumerate(slots):
            at = jnp.where(slot == s, i, at)

        @pl.when(at >= 0)
        def _():
            def add(i, y):
                after[i:] += y.reshape(high - low - i, rows, y.shape[-1])

            lag_chain(dot_nt, near.at[at], kern, p, used[p], low, high, add)

        return carry

    lax.fori_loop(0, kern.shape[0], pair, 0)


def history_front(loc, used, kern, near, before, low, high):
    pairs, lags, panels, _ = kern.shape
    slots = tuple(near)
    blocks = [near[s] for s in slots]
    rows = blocks[0].shape[1]
    share = len(slots) / 12
    return call(
        functools.partial(history_front_body, slots, low, high, before is not None),
        (loc, used),
        [kern] + blocks + ([] if before is None else [before]),
        jax.ShapeDtypeStruct((high - low, rows, panels), F32),
        [pltpu.VMEM((len(slots), lags, rows, panels), BF16)],
        share * 2 * pairs * lags * (high - low) * rows * panels * panels,
        share * 2 * kern.size,
    )


def fill_near(near, own, side, even, odd):
    cuts = even.shape[0]
    near[0] = own[...]
    near[1:cuts] = side[...]
    near[cuts : 2 * cuts] = even[...]
    near[2 * cuts :] = odd[...]


def step_body(n, at, cuts, pairs, has_front, has_back, final, loc, used, *refs):
    refs = list(refs)
    ahead, mine, incoming, inverse, kern = refs[:5]
    moved, refs = refs[5 : 4 + cuts], refs[4 + cuts :]
    total = ahead[at] + mine[...]
    for part in moved:
        total = total + part[...].astype(F32)
    if has_front:
        near = refs[-1]
        fill_near(near, *refs[:4])
        refs = refs[4:]
        for p in range(pairs):
            total = total + dot_nt(near[loc[p]], kern[p, 0])
    if final:
        blocks, rest = refs[: len(final)], refs[-1]
        refs = refs[len(final) :]
        rest[...] = total
        for block, slot in zip(blocks, final):

            def pair(p, carry, block=block, slot=slot):
                @pl.when(loc[p] == slot)
                def _():
                    def add(_, y):
                        rest[...] += y

                    lag_chain(dot_nt, block, kern, p, used[p], 0, 1, add)

                return carry

            lax.fori_loop(0, pairs, pair, 0)
        total = rest[...]
    excess = (incoming[n].astype(F32) - total).astype(BF16)
    density = dot_nt(excess, inverse[...]).astype(BF16)
    if has_back:
        _, out, out_own, out_even, out_odd, sums = refs[:6]
        out[...] = density
        for p in range(pairs):
            sums[loc[p]] += dot_nn(density, kern[p, 0])
        out_own[...] = sums[:cuts]
        out_even[...] = sums[cuts : 2 * cuts].astype(BF16)
        out_odd[...] = sums[2 * cuts :].astype(BF16)
    else:
        earlier, out = refs[: n], refs[n]
        for m in range(n):
            out[m] = earlier[m][...].astype(F32).T.astype(BF16)
        out[n] = density.astype(F32).T.astype(BF16)


def step_call(
    n, steps, loc, used, ahead, mine, moved, incoming, inverse, kern, near, begun, earlier, final
):
    pairs, _, panels, _ = kern.shape
    cuts = len(moved) + 1
    rows = mine.shape[0]
    has_front = near is not None
    has_back = n + 1 < steps
    part = (cuts, rows, panels)
    heap = (3 * cuts, rows, panels)
    ahead, at = ahead
    args = [ahead, mine, incoming, inverse, kern] + moved
    scratch = []
    aliases = {}
    if has_front:
        args += list(near)
    args += list(final.values())
    if has_back:
        args.append(begun)
        outs = (
            jax.ShapeDtypeStruct((rows, panels), BF16),
            jax.ShapeDtypeStruct(part, F32),
            jax.ShapeDtypeStruct(part, BF16),
            jax.ShapeDtypeStruct(part, BF16),
            jax.ShapeDtypeStruct(heap, F32),
        )
        aliases[len(args) - 1] = 4
    else:
        args += earlier
        outs = jax.ShapeDtypeStruct((steps, panels, rows), BF16)
    if has_front:
        scratch.append(pltpu.VMEM(heap, BF16))
    if final:
        scratch.append(pltpu.VMEM((rows, panels), F32))
    return call(
        functools.partial(step_body, n, at, cuts, pairs, has_front, has_back, tuple(final)),
        (loc, used),
        args,
        outs,
        scratch,
        4 * pairs * rows * panels * panels,
        2 * pairs * panels * panels,
        aliases=aliases,
    )


def later_body(back, front, loc, used, kern, *refs):
    refs = list(refs)
    has_near = bool(front)
    near = refs.pop() if has_near else None
    news = refs[len(refs) - len(back) - len(front) :]
    density = refs.pop(0) if back else None
    if has_near:
        fill_near(near, *refs[:4])
        refs = refs[4:]
    rows = [refs[len(back) + i][at] for i, (_, at) in enumerate(front)]
    for p in range(kern.shape[0]):
        slot = loc[p]
        last = used[p]
        for i, lag in enumerate(back):
            news[i][slot] += dot_nn(density[...], gated(kern[p, lag - 1], lag, last))
        for i, (lag, _) in enumerate(front):
            rows[i] += dot_nt(near[slot], gated(kern[p, lag - 1], lag, last))
    for i in range(len(front)):
        news[len(back) + i][0] = rows[i]


def later_call(loc, used, kern, cuts, density, back, near, front):
    pairs, _, panels, _ = kern.shape
    args = [kern]
    scratch = []
    if back:
        args.append(density)
    if front:
        args += list(near)
        scratch.append(pltpu.VMEM((3 * cuts,) + near[0].shape, BF16))
    args += [sums for _, sums in back] + [sums for _, (sums, _) in front]
    rows = (density if back else near[0]).shape[0]
    outs = [jax.ShapeDtypeStruct(sums.shape, F32) for _, sums in back]
    outs += [jax.ShapeDtypeStruct((1, rows, panels), F32) for _ in front]
    terms = len(back) + len(front)
    return call(
        functools.partial(
            later_body, [lag for lag, _ in back], [(lag, at) for lag, (_, at) in front]
        ),
        (loc, used),
        args,
        tuple(outs),
        scratch,
        2 * terms * pairs * rows * panels * panels,
        2 * terms * pairs * panels * panels,
        aliases={len(args) - len(back) - len(front) + i: i for i in range(len(back))},
    )


def gather_near(value):
    cuts = lax.axis_size("cuts")
    side = []
    for j in range(1, cuts):
        side.append(cut_exchange(value, j))
    side = jnp.stack(side)
    region = jnp.concatenate([value[None], side])
    odd = odd_exchange(region)
    even = even_exchange(region)
    return value, side, even, odd


def total_body(own, even, odd, mine, *parts):
    for j in range(own.shape[0]):
        total = own[j] + even[j].astype(F32) + odd[j].astype(F32)
        if j:
            parts[j - 1][...] = total.astype(BF16)
        else:
            mine[...] = total


def sum_parts(own, even, odd):
    cuts = lax.axis_size("cuts")
    odd = odd_exchange(odd)
    even = even_exchange(even)
    mine, *part = call(
        total_body, (), (own, even, odd),
        (jax.ShapeDtypeStruct(own.shape[1:], F32),)
        + (jax.ShapeDtypeStruct(own.shape[1:], BF16),) * (cuts - 1),
        [], 2 * own.size, 8 * own.size,
    )
    moved = []
    for j in range(1, cuts):
        moved.append(cut_exchange(part[j - 1], j))
    return mine, moved


def every_step(history, incident, self_inverse, lag_kernels, pair_partner, pair_lags):
    steps = incident.shape[0]
    cuts = lax.axis_size("cuts")
    hist, loc, used = enter(pair_partner, pair_lags, history, cuts)
    incoming = turned(incident)

    half = pair_lags.shape[0] // 2
    heaps = history_back(loc, used, hist, lag_kernels, cuts, steps, 0, half, None)
    *heaps, own, even, odd = history_back(
        loc, used, hist, lag_kernels, cuts, steps, half, pair_lags.shape[0], heaps
    )
    begun = {steps - 1 - i: heap for i, heap in enumerate(heaps)}
    mine, moved = sum_parts(own, even, odd)

    pieces = {0: hist, **cut_pieces(hist)}
    blocks = {}
    for j, piece in pieces.items():
        odd = odd_exchange(piece)
        even = even_exchange(piece)
        blocks.update({j: piece, cuts + j: even, 2 * cuts + j: odd})
    *_, j_final = pieces
    final = {slot: blocks.pop(slot) for slot in range(cuts + j_final, 3 * cuts, cuts)}
    early = {*range(cuts), cuts, 2 * cuts} - {j_final}
    late = {slot: block for slot, block in blocks.items() if slot not in early}
    blocks = {slot: block for slot, block in blocks.items() if slot in early}
    sums = history_front(loc, used, lag_kernels, blocks, None, 0, steps)
    sums = history_front(loc, used, lag_kernels, late, sums, 0, steps)
    ahead = {n: (sums, steps - 1 - n) for n in range(steps)}

    near = None
    densities = []
    for n in range(steps - 1):
        density, own, even, odd, _ = step_call(
            n, steps, loc, used, ahead[n], mine, moved, incoming, self_inverse, lag_kernels,
            near, begun.get(n + 1), None, {} if n else final,
        )
        densities.append(density)
        before, near = near, gather_near(density)
        mine, moved = sum_parts(own, even, odd)
        if n == 0:
            sums = history_front(loc, used, lag_kernels, final, sums, 1, steps)
            ahead = {m: (sums, steps - 1 - m) for m in range(1, steps)}
        back = [(m - n, begun[m]) for m in range(n + 2, steps)]
        front = [(m - n + 1, ahead[m]) for m in range(n + 1, steps)] if n else []
        if back or front:
            news = later_call(loc, used, lag_kernels, cuts, density, back, before, front)
            for i, m in enumerate(range(n + 2, steps)):
                begun[m] = news[i]
            if n:
                for i, m in enumerate(range(n + 1, steps)):
                    ahead[m] = (news[len(back) + i], 0)
    return step_call(
        steps - 1, steps, loc, used, ahead[steps - 1], mine, moved, incoming, self_inverse,
        lag_kernels, near, None, densities, {},
    )


def solution(mesh):
    return jax.shard_map(
        every_step,
        mesh=mesh,
        in_specs=(
            P(None, ("region", "cuts"), None),
            P(None, ("region", "cuts"), None),
            P(("region", "cuts"), None),
            P(("region", "cuts"), None, None, None),
            P(("region", "cuts")),
            P(("region", "cuts")),
        ),
        out_specs=P(None, ("region", "cuts"), None),
        check_vma=False,
    )
```
